32 devices in a mesh: seq: 8 (over z, y), dp: 4 (over x, core).
Axes of the slice: x: 2, y: 2, z: 4, core: 2. Of those that a mesh axis runs over, the one named last changes fastest.
Arguments:
- byte_states: bfloat16 [4, 2048, 4096], P('dp', 'seq'), may hold values from -16 to 16
- byte_patch: int32 [4, 2048], P('dp', 'seq'), may hold values from 0 to 575, as said below
- patch_owner: int32 [4, 576], P('dp'), may hold values from 0 to 7, as said below
- qkv_weight: bfloat16 [4096, 3072], P(None, 'dp'), may hold values from -0.09375 to 0.09375
- attention_output_gradient: bfloat16 [4, 576, 2048], P('dp', 'seq'), may hold values from -6 to 6
Outputs:
- attention: bfloat16 [4, 576, 2048], P('dp', 'seq')
- state_grad: bfloat16 [4, 2048, 4096], P('dp', 'seq')
- weight_grad: float32 [4096, 3072], P('seq', 'dp')
The draws below stay inside these ranges and needn't reach their ends.
Inputs may be any that keep to these rules, and one draw needn't show every extreme that they name: `byte_patch`: patch numbers never fall along a sequence, every patch lies within the bytes of one index of seq, and every patch number is used. One index of seq in each sequence, drawn, holds 128 patches of two bytes; every other index holds 64 patches in consecutive pairs that together hold 8 bytes, each patch 1 to 7 bytes. `patch_owner`: patches 0 to 7, 8 to 15 and so on form groups in which every owner appears exactly once.
All inputs are finite; a program needn't handle non-finite values.
Results may differ from the reference program's by a relative error of at most 0.028.
Values may be sent and summed in bfloat16 or wider, within the bound.
No kernel may reach another device: no remote copies, remote signals or barrier semaphores. Data moves between devices by JAX's collectives and lax.ppermute only.
A program may use at most 128 MiB of HBM per device.

```python
import jax
import jax.numpy as jnp
from jax import lax

DG = 4096
QUERY_HEADS = 16
KEY_VALUE_HEADS = 4
HEAD_SIZE = 128
PIECE_CHARACTERS = 256
STRAND_TALLY = 4
LEN = 2048
SEQUENCE_PATCHES = 576
OWNER_PATCHES = 72
QKV = 3072
COLS = 768
N_SEQ = 8
N_DP = 4


def patch_layout(key):
    spike_piece_position = jax.random.randint(jax.random.fold_in(key, 11), (STRAND_TALLY,), 0, N_SEQ)
    firsts = jax.random.randint(jax.random.fold_in(key, 12), (STRAND_TALLY, N_SEQ, PIECE_CHARACTERS // 8), 1, 8)
    beginning_displacements = jnp.arange(PIECE_CHARACTERS, dtype=jnp.int32)
    pair_index = beginning_displacements // 8
    within = beginning_displacements % 8
    gaussian_draw = 2 * pair_index[None, None, :] + (within[None, None, :] >= firsts[:, :, pair_index]).astype(jnp.int32)
    spike_member_entries = beginning_displacements // 2
    piece_tally = jnp.arange(N_SEQ, dtype=jnp.int32)
    within_spike = piece_tally[None, :] == spike_piece_position[:, None]
    foremost_entry = piece_tally[None, :] * (PIECE_CHARACTERS // 4) + (piece_tally[None, :] > spike_piece_position[:, None]).astype(jnp.int32) * (PIECE_CHARACTERS // 4)
    hosted_segment = jnp.where(within_spike[:, :, None], spike_member_entries[None, None, :], gaussian_draw)
    byte_patch = (foremost_entry[:, :, None] + hosted_segment).reshape(STRAND_TALLY, LEN).astype(jnp.int32)
    ranked = jax.random.randint(jax.random.fold_in(key, 13), (STRAND_TALLY, OWNER_PATCHES, N_SEQ), 0, 1 << 20) * N_SEQ + piece_tally[None, None, :]
    owner_order = jnp.argsort(ranked, axis=-1, stable=True).astype(jnp.int32)
    return (byte_patch, owner_order.reshape(STRAND_TALLY, SEQUENCE_PATCHES))


def draw_byte_patch(key, part):
    return patch_layout(key)[0]


def draw_patch_owner(key, part):
    return patch_layout(key)[1]


def draw_byte_states(key, part):
    key_noise = jax.random.fold_in(key, 21)
    value_rows = jnp.clip(jax.random.normal(key_noise, (STRAND_TALLY, LEN, DG), jnp.float32), -6.0, 6.0)
    return jnp.clip(value_rows, -16.0, 16.0).astype(jnp.bfloat16)


def levels(key, shape, cuts, low, high):
    gain, own = 1.0, jax.random.fold_in(key, 6)
    for position, parts in cuts:
        draws = jnp.exp(jax.random.uniform(jax.random.fold_in(own, position), (parts,), jnp.float32, low / len(cuts), high / len(cuts)))
        gain = gain * jnp.repeat(draws, shape[position] // parts).reshape([-1 if axis == position else 1 for axis in range(len(shape))])
    return gain


def scatter_about(own_key, extent, width, reach, cuts=(), kind=jnp.bfloat16):
    array = jax.random.normal(own_key, extent, jnp.float32) * width
    if len(cuts) > 0:
        array = levels(own_key, extent, cuts, -0.22, 0.18) * array
    return jnp.clip(array, min=-reach, max=reach).astype(kind)


def setup_inputs(seed: int = 0) -> dict:
    seeds = jax.random.split(jax.random.key(seed), 6)
    return {
        "byte_states": draw_byte_states(jax.random.fold_in(seeds[5], 71), 0),
        "byte_patch": draw_byte_patch(jax.random.fold_in(seeds[5], 71), 0),
        "patch_owner": draw_patch_owner(jax.random.fold_in(seeds[5], 71), 0),
        "qkv_weight": scatter_about(seeds[3], (DG, QKV), DG ** -0.5, 0.09375, ((1, 4),)),
        "attention_output_gradient": scatter_about(seeds[4], (STRAND_TALLY, SEQUENCE_PATCHES, QUERY_HEADS * HEAD_SIZE), 1.0, 6.0, ((0, 4), (1, 8))),
    }


def contract_rows(left, right):
    return lax.dot_general(left, right, (((0,), (0,)), ((), ())), preferred_element_type=jnp.float32)


def one_sequence(states, patch_ids, owners, qkv_weight, output_cotangent):
    unit_terms = jnp.ones((LEN,), jnp.float32)
    counts = jax.ops.segment_sum(unit_terms, patch_ids, num_segments=SEQUENCE_PATCHES)
    summed = jax.ops.segment_sum(states.astype(jnp.float32), patch_ids, num_segments=SEQUENCE_PATCHES)
    pooled = (summed / jnp.maximum(counts, 1.0)[:, None]).astype(jnp.bfloat16)
    patch_order = jnp.arange(SEQUENCE_PATCHES, dtype=jnp.int32)
    placed = (owners * OWNER_PATCHES + patch_order // N_SEQ).astype(jnp.int32)
    own_rows = jnp.zeros_like(pooled).at[placed].set(pooled)
    own_index = jnp.zeros((SEQUENCE_PATCHES,), jnp.int32).at[placed].set(patch_order)
    projected_states = jnp.dot(own_rows, qkv_weight, preferred_element_type=jnp.float32).astype(jnp.bfloat16)
    query_group_size = QUERY_HEADS // KEY_VALUE_HEADS
    query_row_width = QUERY_HEADS * HEAD_SIZE
    key_row_width = KEY_VALUE_HEADS * HEAD_SIZE
    query_rows = projected_states[:, :query_row_width].reshape(SEQUENCE_PATCHES, KEY_VALUE_HEADS, query_group_size, HEAD_SIZE).astype(jnp.float32)
    key_head_count = projected_states[:, query_row_width:query_row_width + key_row_width].reshape(SEQUENCE_PATCHES, KEY_VALUE_HEADS, HEAD_SIZE).astype(jnp.float32)
    value_rows = projected_states[:, query_row_width + key_row_width:].reshape(SEQUENCE_PATCHES, KEY_VALUE_HEADS, HEAD_SIZE).astype(jnp.float32)
    factor = HEAD_SIZE ** -0.5
    scores = jnp.einsum('qhgd,khd->hgqk', query_rows, key_head_count) * factor
    allowed = own_index[None, :] <= own_index[:, None]
    scores = jnp.where(allowed[None, None], scores, -jnp.inf)
    row_peak = jnp.max(scores, axis=-1, keepdims=True)
    shifted = jnp.exp(scores - row_peak)
    attend = shifted / jnp.sum(shifted, axis=-1, keepdims=True)
    attended_lower = attend.astype(jnp.bfloat16).astype(jnp.float32)
    attended = jnp.einsum('hgqk,khd->qhgd', attended_lower, value_rows)
    attention = attended.reshape(SEQUENCE_PATCHES, query_row_width).astype(jnp.bfloat16)
    gradient_row_list = output_cotangent.astype(jnp.float32).reshape(SEQUENCE_PATCHES, KEY_VALUE_HEADS, query_group_size, HEAD_SIZE)
    grad_attend = jnp.einsum('qhgd,khd->hgqk', gradient_row_list, value_rows)
    row_delta = jnp.einsum('qhgd,qhgd->hgq', gradient_row_list, attended)
    score_gradient = (attend * (grad_attend - row_delta[..., None])).astype(jnp.bfloat16).astype(jnp.float32)
    grad_queries = jnp.einsum('hgqk,khd->qhgd', score_gradient, key_head_count) * factor
    score_block_list = score_gradient.reshape(KEY_VALUE_HEADS, query_group_size, N_SEQ, OWNER_PATCHES, SEQUENCE_PATCHES)
    attended_block_list = attended_lower.reshape(KEY_VALUE_HEADS, query_group_size, N_SEQ, OWNER_PATCHES, SEQUENCE_PATCHES)
    query_block_list = query_rows.reshape(N_SEQ, OWNER_PATCHES, KEY_VALUE_HEADS, query_group_size, HEAD_SIZE)
    gradient_block_list = gradient_row_list.reshape(N_SEQ, OWNER_PATCHES, KEY_VALUE_HEADS, query_group_size, HEAD_SIZE)
    key_part = (jnp.einsum('hgiqk,iqhgd->ikhd', score_block_list, query_block_list) * factor).astype(jnp.bfloat16).astype(jnp.float32)
    grad_keys = jnp.sum(key_part, axis=0)
    value_part = jnp.einsum('hgiqk,iqhgd->ikhd', attended_block_list, gradient_block_list).astype(jnp.bfloat16).astype(jnp.float32)
    grad_values = jnp.sum(value_part, axis=0)
    grad_proj = jnp.concatenate([grad_queries.reshape(SEQUENCE_PATCHES, query_row_width), grad_keys.reshape(SEQUENCE_PATCHES, key_row_width), grad_values.reshape(SEQUENCE_PATCHES, key_row_width)], axis=1).astype(jnp.bfloat16)
    grad_split = grad_proj.reshape(SEQUENCE_PATCHES, N_DP, COLS).astype(jnp.float32)
    weight_split = qkv_weight.reshape(DG, N_DP, COLS).astype(jnp.float32)
    pooled_part = jnp.einsum('pic,gic->ipg', grad_split, weight_split).astype(jnp.bfloat16).astype(jnp.float32)
    grad_pooled = jnp.sum(pooled_part, axis=0).astype(jnp.bfloat16)
    per_patch = grad_pooled[placed].astype(jnp.float32) / jnp.maximum(counts, 1.0)[:, None]
    state_grad = per_patch[patch_ids].astype(jnp.bfloat16)
    return attention, state_grad, own_rows, grad_proj


def reference(byte_states, byte_patch, patch_owner, qkv_weight, attention_output_gradient):
    outputs = []
    grads = []
    row_list = []
    proj_list = []
    for index_seq in range(STRAND_TALLY):
        attention, state_grad, own_rows, grad_proj = one_sequence(byte_states[index_seq], byte_patch[index_seq], patch_owner[index_seq], qkv_weight, attention_output_gradient[index_seq])
        outputs.append(attention)
        grads.append(state_grad)
        row_list.append(own_rows)
        proj_list.append(grad_proj)
    row_blocks = jnp.stack(row_list).reshape(STRAND_TALLY, N_SEQ, OWNER_PATCHES, DG).transpose(1, 0, 2, 3).reshape(N_SEQ, STRAND_TALLY * OWNER_PATCHES, DG)
    proj_blocks = jnp.stack(proj_list).reshape(STRAND_TALLY, N_SEQ, OWNER_PATCHES, QKV).transpose(1, 0, 2, 3).reshape(N_SEQ, STRAND_TALLY * OWNER_PATCHES, QKV)

    def add_block(total, pair):
        term = contract_rows(pair[0], pair[1]).astype(jnp.bfloat16).astype(jnp.float32)
        return total + term, None

    weight_grad, unused = lax.scan(add_block, jnp.zeros((DG, QKV), jnp.float32), (row_blocks, proj_blocks))
    return jnp.stack(outputs), jnp.stack(grads), weight_grad
```

```python
import functools

import jax
import jax.numpy as jnp
from jax import lax
from jax.experimental import pallas as pl
from jax.experimental.pallas import tpu as pltpu
from jax.sharding import PartitionSpec as P

QUERY_HEADS = 16
KEY_VALUE_HEADS = 4
HEAD_SIZE = 128
BF = jnp.bfloat16
F32 = jnp.float32


def dot(left, right, dims):
    return lax.dot_general(left, right, (dims, ((), ())), preferred_element_type=F32)


def attention_kernel(
    n, base, extra, heads, splits, block,
    spike_ref, unit_ref, target_ref, qkv_ref, cot_ref, out_ref, grad_ref,
    cot_scratch, out_scratch, key_scratch, value_scratch,
):
    rows = base + extra
    total = qkv_ref.shape[0]
    width = heads * HEAD_SIZE
    factor = HEAD_SIZE ** (-0.5)
    spike = spike_ref[0]

    def patch_of(position):
        holder = jnp.zeros_like(position)
        for k in range(1, n):
            holder = holder + (position >= k * rows).astype(jnp.int32)
        slot = position - holder * rows
        plain = base * (holder + (holder > spike).astype(jnp.int32)) + slot
        spread = base * (spike + 1) + holder * extra + (slot - base)
        return jnp.where(slot < base, plain, spread)

    lanes = lax.broadcasted_iota(jnp.int32, (1, total), 1)
    patch_row = patch_of(lanes)

    for start in range(0, total, block):
        pick = (target_ref[start : start + block, :] == lanes).astype(BF)
        cot_scratch[start : start + block, :] = dot(
            pick, cot_ref[...], ((1,), (0,))
        ).astype(BF)

    keys = qkv_ref[:, width : width + HEAD_SIZE]
    values = qkv_ref[:, width + HEAD_SIZE : width + 2 * HEAD_SIZE]
    for start in range(0, total, block):
        stop = start + block
        position = start + lax.broadcasted_iota(jnp.int32, (block, 1), 0)
        patch_col = patch_of(position)
        allowed = patch_row <= patch_col
        pick = (patch_col == lanes).astype(BF)
        cot = dot(pick, cot_scratch[...], ((1,), (0,))).astype(BF)
        outs = []
        for head in range(heads):
            cols = slice(head * HEAD_SIZE, (head + 1) * HEAD_SIZE)
            query = qkv_ref[start:stop, cols]
            scores = dot(query, keys, ((1,), (1,))) * factor
            scores = jnp.where(allowed, scores, -jnp.inf)
            peak = jnp.max(scores, axis=-1, keepdims=True)
            shifted = jnp.exp(scores - peak)
            attend = shifted / jnp.sum(shifted, axis=-1, keepdims=True)
            if splits > 1:
                part = (position * splits) // total
                attend = jnp.where(part == unit_ref[0] % splits, attend, 0.0)
            low = attend.astype(BF)
            attended = dot(low, values, ((1,), (0,)))
            outs.append(attended.astype(BF))
            cot_head = cot[:, cols]
            grad_attend = dot(cot_head, values, ((1,), (1,)))
            delta = jnp.sum(cot_head.astype(F32) * attended, axis=-1, keepdims=True)
            score_grad = (attend * (grad_attend - delta)).astype(BF)
            grad_ref[start:stop, cols] = (
                dot(score_grad, keys, ((1,), (0,))) * factor
            ).astype(BF)
            key_term = dot(score_grad, query, ((0,), (0,)))
            value_term = dot(low, cot_head, ((0,), (0,)))
            if start == 0 and head == 0:
                key_scratch[...] = key_term
                value_scratch[...] = value_term
            else:
                key_scratch[...] += key_term
                value_scratch[...] += value_term
        term = dot(pick, jnp.concatenate(outs, axis=1), ((0,), (0,)))
        if start == 0:
            out_scratch[...] = term
        else:
            out_scratch[...] += term
    grad_ref[:, width : width + HEAD_SIZE] = (key_scratch[...] * factor).astype(BF)
    grad_ref[:, width + HEAD_SIZE :] = value_scratch[...].astype(BF)
    placed = out_scratch[...].astype(BF)
    for start in range(0, total, block):
        pick = (target_ref[start : start + block, :] == lanes).astype(BF)
        term = dot(pick, placed[start : start + block, :], ((0,), (0,)))
        if start == 0:
            out_scratch[...] = term
        else:
            out_scratch[...] += term
    out_ref[...] = out_scratch[...].astype(BF)


def attention_call(n, base, extra, heads, splits, spike, unit, target, qkv, cot):
    total, wide = qkv.shape
    width = heads * HEAD_SIZE
    block = max(b for b in range(16, 193, 16) if total % b == 0)
    vmem = pl.BlockSpec(memory_space=pltpu.VMEM)
    smem = pl.BlockSpec(memory_space=pltpu.SMEM)
    return pl.pallas_call(
        functools.partial(attention_kernel, n, base, extra, heads, splits, block),
        out_shape=(
            jax.ShapeDtypeStruct((total, width), BF),
            jax.ShapeDtypeStruct((total, wide), BF),
        ),
        in_specs=[smem, smem, vmem, vmem, vmem],
        out_specs=(vmem, vmem),
        scratch_shapes=[
            pltpu.VMEM((total, width), BF),
            pltpu.VMEM((total, width), F32),
            pltpu.VMEM((total, HEAD_SIZE), F32),
            pltpu.VMEM((total, HEAD_SIZE), F32),
        ],
        compiler_params=pltpu.CompilerParams(vmem_limit_bytes=48 * 1024 * 1024),
        name="attention",
    )(spike, unit, target, qkv, cot)


def body(byte_states, byte_patch, patch_owner, qkv_weight, attention_output_gradient):
    n, nd = lax.axis_size("seq"), lax.axis_size("dp")
    nx = nd // 2
    column_index = lax.axis_index("dp")
    seq_index = lax.axis_index("seq")
    ny = 1
    while 2 * (2 * ny) ** 2 <= n:
        ny *= 2
    nz = n // ny

    byte_rows = byte_states[0]
    byte_total, model = byte_rows.shape
    slot_count = byte_total // 2
    base = byte_total // 4
    owner_rows = attention_output_gradient.shape[1]
    extra = owner_rows - base
    total = patch_owner.shape[1]
    columns = qkv_weight.shape[1]

    def dp_hop(value, distance):
        return lax.ppermute(value, "dp", [(i, i ^ distance) for i in range(nd)])

    def seq_swap(value):
        return lax.all_to_all(value, "seq", split_axis=0, concat_axis=0, tiled=True)

    def dp_gather(value):
        blocks = [None] * nd
        blocks[0] = value
        for k in range(1, nx):
            blocks[2 * k] = dp_hop(value, 2 * k)
        for k in range(nx):
            blocks[2 * k + 1] = dp_hop(blocks[2 * k], 1)
        return blocks

    def dp_swap(blocks):
        across = [None] * nx
        across[0] = (blocks[0], blocks[1])
        for k in range(1, nx):
            got = dp_hop(jnp.stack([blocks[2 * k], blocks[2 * k + 1]]), 2 * k)
            across[k] = (got[0], got[1])
        result = [None] * nd
        first = dp_hop(across[0][1], 1)
        rest = dp_hop(jnp.stack([across[k][1] for k in range(1, nx)]), 1)
        for k in range(nx):
            result[2 * k] = across[k][0]
            result[2 * k + 1] = first if k == 0 else rest[k - 1]
        return result

    def dp_reduce(value):
        pairs = value.reshape((nx, 2) + value.shape[1:])
        got = dp_hop(pairs[:, 1], 1)
        held = (pairs[:, 0].astype(F32) + got.astype(F32)).astype(BF)
        result = held[0].astype(F32)
        for k in range(1, nx):
            result = result + dp_hop(held[k], 2 * k).astype(F32)
        return result.astype(BF)

    patch_ids = byte_patch[0]
    first_patch = patch_ids[0]
    local_ids = patch_ids - first_patch
    slot_range = jnp.arange(slot_count, dtype=jnp.int32)
    onehot = local_ids[None, :] == slot_range[:, None]
    counts = jnp.sum(onehot.astype(F32), axis=1)
    summed = dot(onehot.astype(BF), byte_rows, ((1,), (0,)))
    pooled = (summed / jnp.maximum(counts, 1.0)[:, None]).astype(BF)
    base_rows = pooled[:base]
    spread = seq_swap(pooled[base:].reshape(n, extra, model))
    extra_rows = jnp.sum(spread.astype(F32), axis=0).astype(BF)

    base_all = jnp.concatenate(dp_gather(base_rows), axis=0)
    extra_all = jnp.concatenate(dp_gather(extra_rows), axis=0)
    proj_base = dot(base_all, qkv_weight, ((1,), (0,))).astype(BF).reshape(nd, base, columns)
    proj_extra = dot(extra_all, qkv_weight, ((1,), (0,))).astype(BF).reshape(nd, extra, columns)
    proj = jnp.concatenate([proj_base, proj_extra], axis=1)

    relative = jnp.stack(dp_swap([proj[r] for r in range(nd)]))
    projected = jnp.concatenate(
        [
            lax.dynamic_index_in_dim(relative, column_index ^ k, 0, keepdims=False)
            for k in range(nd)
        ],
        axis=1,
    )

    heads = max(1, QUERY_HEADS // n)
    splits = max(1, n // QUERY_HEADS)
    width = heads * HEAD_SIZE
    query_width = QUERY_HEADS * HEAD_SIZE
    key_width = KEY_VALUE_HEADS * HEAD_SIZE
    group = QUERY_HEADS // KEY_VALUE_HEADS

    def query_of(unit):
        return (unit // splits) * width

    def key_of(unit):
        return query_width + (unit // splits) * heads // group * HEAD_SIZE

    sends = []
    for unit in range(n):
        q, k = query_of(unit), key_of(unit)
        sends.append(
            jnp.concatenate(
                [
                    projected[:, q : q + width],
                    projected[:, k : k + HEAD_SIZE],
                    projected[:, k + key_width : k + key_width + HEAD_SIZE],
                ],
                axis=1,
            )
        )
    qkv = seq_swap(jnp.stack(sends)).reshape(total, width + 2 * HEAD_SIZE)

    cotangent = attention_output_gradient[0]
    behind = (first_patch // base - seq_index).astype(BF)
    flags = jnp.broadcast_to(behind, (n, 8, width))
    cot_sends = jnp.stack(
        [cotangent[:, query_of(unit) : query_of(unit) + width] for unit in range(n)]
    )
    cot_got = seq_swap(jnp.concatenate([cot_sends, flags], axis=1))
    cot = cot_got[:, :owner_rows].reshape(total, width)
    after = jnp.sum(cot_got[:, owner_rows, 0].astype(F32)).astype(jnp.int32)
    spike = n - 1 - after

    patch_range = jnp.arange(total, dtype=jnp.int32)
    target = (patch_owner[0] * owner_rows + patch_range // n)[:, None]
    out_rows, grads = attention_call(
        n, base, extra, heads, splits,
        spike.reshape(1), seq_index.astype(jnp.int32).reshape(1), target, qkv, cot,
    )

    out_got = seq_swap(out_rows.reshape(n, owner_rows, width))
    if splits > 1:
        out_got = jnp.sum(
            out_got.astype(F32).reshape(n // splits, splits, owner_rows, width), axis=1
        ).astype(BF)
    attn = jnp.concatenate([out_got[u] for u in range(n // splits)], axis=1)

    grads_got = seq_swap(grads.reshape(n, owner_rows, width + 2 * HEAD_SIZE))
    pieces = []
    for unit in range(0, n, splits):
        piece = grads_got[unit, :, :width]
        if splits > 1:
            piece = jnp.sum(
                grads_got[unit : unit + splits, :, :width].astype(F32), axis=0
            ).astype(BF)
        pieces.append(piece)
    per_key = n // KEY_VALUE_HEADS
    for offset in (width, width + HEAD_SIZE):
        for head in range(KEY_VALUE_HEADS):
            part = grads_got[
                head * per_key : (head + 1) * per_key, :, offset : offset + HEAD_SIZE
            ]
            pieces.append(jnp.sum(part.astype(F32), axis=0).astype(BF))
    grad_proj = jnp.concatenate(pieces, axis=1)
    grad_blocks = jnp.stack(
        [grad_proj[:, k * columns : (k + 1) * columns] for k in range(nd)]
    )
    grad_cols = jnp.stack(
        dp_swap(
            [
                lax.dynamic_index_in_dim(grad_blocks, column_index ^ r, 0, keepdims=False)
                for r in range(nd)
            ]
        )
    )

    back_extra = dot(
        grad_cols[:, base:].reshape(nd * extra, columns), qkv_weight, ((1,), (1,))
    ).astype(BF)
    extra_grad = dp_reduce(back_extra.reshape(nd, extra, model))
    to_spike = (jnp.arange(n, dtype=jnp.int32) == spike)[:, None, None]
    extra_back = seq_swap(jnp.where(to_spike, extra_grad[None], jnp.zeros((), BF)))
    back_base = dot(
        grad_cols[:, :base].reshape(nd * base, columns), qkv_weight, ((1,), (1,))
    ).astype(BF)
    base_grad = dp_reduce(back_base.reshape(nd, base, model))
    slot_grads = jnp.concatenate([base_grad, extra_back.reshape(base, model)], axis=0)
    byte_counts = jnp.sum(jnp.where(onehot, counts[:, None], 0.0), axis=0)
    picked = dot(onehot.astype(BF), slot_grads, ((0,), (0,)))
    state_grad = (picked / jnp.maximum(byte_counts, 1.0)[:, None]).astype(BF)

    own_rows = jnp.concatenate([base_rows, extra_rows], axis=0)
    strip = model // n
    strips = seq_swap(
        jnp.stack([own_rows[:, k * strip : (k + 1) * strip] for k in range(n)])
    )
    all_strips = jnp.stack(dp_gather(strips), axis=1)
    zi, yi = seq_index // ny, seq_index % ny
    current = grad_cols.reshape(nd * owner_rows, columns)
    weight_grad = jnp.zeros((strip, columns), F32)
    for kz in range(nz):
        for ky in range(ny):
            moved = current
            if ky:
                moved = lax.ppermute(
                    current,
                    "seq",
                    [(z * ny + y, z * ny + (y + ky) % ny) for z in range(nz) for y in range(ny)],
                )
            source = ((zi - kz) % nz) * ny + (yi - ky) % ny
            left = lax.dynamic_index_in_dim(all_strips, source, 0, keepdims=False)
            weight_grad = weight_grad + dot(
                left.reshape(nd * owner_rows, strip), moved, ((0,), (0,))
            )
        if kz < nz - 1:
            current = lax.ppermute(
                current,
                "seq",
                [(z * ny + y, ((z + 1) % nz) * ny + y) for z in range(nz) for y in range(ny)],
            )
    return (attn[None], state_grad[None], weight_grad)


def solution(mesh):
    return jax.shard_map(
        body,
        mesh=mesh,
        in_specs=(
            P("dp", "seq", None),
            P("dp", "seq"),
            P("dp", None),
            P(None, "dp"),
            P("dp", "seq", None),
        ),
        out_specs=(P("dp", "seq", None), P("dp", "seq", None), P("seq", "dp")),
        check_vma=False,
    )
```

```python
import functools

import jax
import jax.numpy as jnp
from jax import lax
from jax.experimental import pallas as pl
from jax.experimental.pallas import tpu as pltpu
from jax.sharding import PartitionSpec as P


QUERY_HEADS = 16
KEY_VALUE_HEADS = 4
HEAD_SIZE = 128
BF = jnp.bfloat16
F32 = jnp.float32


def dot(left, right, dims):
    return lax.dot_general(left, right, (dims, ((), ())), preferred_element_type=F32)


def attention_kernel(
    n, base, extra, heads, splits, block, unit_ref, target_ref, cot_ref, *refs
):
    qkv_refs, grad_refs = refs[:n], refs[n + 1 : 2 * n + 1]
    out_ref, spike_ref = refs[n], refs[2 * n + 1]
    qkv_scratch, qkv_ref, cot_scratch, out_scratch, grad_scratch, key_scratch, value_scratch = (
        refs[2 * n + 2 :]
    )
    rows = base + extra
    total = qkv_ref.shape[0]
    width = heads * HEAD_SIZE
    factor = HEAD_SIZE ** (-0.5)
    unit = unit_ref[0]
    padded = cot_ref.shape[0] // n
    after = jnp.zeros((1, HEAD_SIZE), F32)
    for k in range(n):
        qkv_scratch[k * rows : (k + 1) * rows, :] = qkv_refs[k][...].astype(F32)
        flag = k * padded + rows
        after = after + cot_ref[flag : flag + 1, :HEAD_SIZE].astype(F32)
    qkv_ref[...] = qkv_scratch[...].astype(BF)
    spike_ref[...] = jnp.broadcast_to((n - 1) - after.astype(jnp.int32), spike_ref.shape)
    spike = spike_ref[0:1, 0:1]
    every = lax.broadcasted_iota(jnp.int32, (1, n * padded), 1)

    def patch_of(position):
        place = jnp.zeros_like(position)
        for k in range(1, n):
            place = place + (position >= k * rows).astype(jnp.int32)
        slot = position - place * rows
        holder = place ^ unit
        plain = base * (holder + (holder > spike).astype(jnp.int32)) + slot
        spread = base * (spike + 1) + holder * extra + (slot - base)
        return jnp.where(slot < base, plain, spread)

    lanes = lax.broadcasted_iota(jnp.int32, (1, total), 1)
    patch_row = patch_of(lanes)

    for start in range(0, total, block):
        pick = (target_ref[start : start + block, 0:1] == every).astype(BF)
        cot_scratch[start : start + block, :] = dot(
            pick, cot_ref[...], ((1,), (0,))
        ).astype(BF)

    keys = qkv_ref[:, width : width + HEAD_SIZE]
    values = qkv_ref[:, width + HEAD_SIZE : width + 2 * HEAD_SIZE]
    for start in range(0, total, block):
        stop = start + block
        position = start + lax.broadcasted_iota(jnp.int32, (block, 1), 0)
        patch_col = patch_of(position)
        allowed = patch_row <= patch_col
        pick = (patch_col == lanes).astype(BF)
        cot = dot(pick, cot_scratch[...], ((1,), (0,))).astype(BF)
        outs = []
        for head in range(heads):
            cols = slice(head * HEAD_SIZE, (head + 1) * HEAD_SIZE)
            query = qkv_ref[start:stop, cols]
            scores = dot(query, keys, ((1,), (1,))) * factor
            scores = jnp.where(allowed, scores, -jnp.inf)
            peak = jnp.max(scores, axis=-1, keepdims=True)
            shifted = jnp.exp(scores - peak)
            attend = shifted / jnp.sum(shifted, axis=-1, keepdims=True)
            if splits > 1:
                part = (position * splits) // total
                attend = jnp.where(part == unit % splits, attend, 0.0)
            low = attend.astype(BF)
            attended = dot(low, values, ((1,), (0,)))
            outs.append(attended.astype(BF))
            cot_head = cot[:, cols]
            grad_attend = dot(cot_head, values, ((1,), (1,)))
            delta = jnp.sum(cot_head.astype(F32) * attended, axis=-1, keepdims=True)
            score_grad = (attend * (grad_attend - delta)).astype(BF)
            grad_scratch[start:stop, cols] = dot(score_grad, keys, ((1,), (0,))) * factor
            key_term = dot(score_grad, query, ((0,), (0,)))
            value_term = dot(low, cot_head, ((0,), (0,)))
            if start == 0 and head == 0:
                key_scratch[...] = key_term
                value_scratch[...] = value_term
            else:
                key_scratch[...] += key_term
                value_scratch[...] += value_term
        term = dot(pick, jnp.concatenate(outs, axis=1), ((0,), (0,)))
        if start == 0:
            out_scratch[...] = term
        else:
            out_scratch[...] += term
    for k in range(n):
        part = slice(k * rows, (k + 1) * rows)
        grad_refs[k][:, :width] = grad_scratch[part, :].astype(BF)
        grad_refs[k][:, width : width + HEAD_SIZE] = (key_scratch[part, :] * factor).astype(BF)
        grad_refs[k][:, width + HEAD_SIZE :] = value_scratch[part, :].astype(BF)
    placed = out_scratch[...].astype(BF)
    for start in range(0, total, block):
        pick = (target_ref[start : start + block, 1:2] == lanes).astype(BF)
        term = dot(pick, placed[start : start + block, :], ((0,), (0,)))
        if start == 0:
            out_scratch[...] = term
        else:
            out_scratch[...] += term
    out_ref[...] = out_scratch[...].astype(BF)


def attention_call(n, base, extra, heads, splits, unit, target, cot, qkvs):
    rows, wide = qkvs[0].shape
    total = n * rows
    width = heads * HEAD_SIZE
    block = max(b for b in range(16, 193, 16) if total % b == 0)
    vmem = pl.BlockSpec(memory_space=pltpu.VMEM)
    smem = pl.BlockSpec(memory_space=pltpu.SMEM)
    return pl.pallas_call(
        functools.partial(attention_kernel, n, base, extra, heads, splits, block),
        out_shape=[jax.ShapeDtypeStruct((total, width), BF)]
        + [jax.ShapeDtypeStruct((rows, wide), BF)] * n
        + [jax.ShapeDtypeStruct((8, HEAD_SIZE), jnp.int32)],
        in_specs=[smem] + [vmem] * (2 + n),
        out_specs=[vmem] * (n + 2),
        scratch_shapes=[
            pltpu.VMEM((total, wide), F32),
            pltpu.VMEM((total, wide), BF),
            pltpu.VMEM((total, width), BF),
            pltpu.VMEM((total, width), F32),
            pltpu.VMEM((total, width), F32),
            pltpu.VMEM((total, HEAD_SIZE), F32),
            pltpu.VMEM((total, HEAD_SIZE), F32),
        ],
        compiler_params=pltpu.CompilerParams(
            vmem_limit_bytes=(16 if total < 1024 else 48) * 1024 * 1024
        ),
        name="attention",
    )(unit, target, cot, *qkvs)


def send_kernel(n, heads, splits, index_ref, *refs):
    nd = len(refs) - n - 1
    blocks, outs, whole = refs[:nd], refs[nd : nd + n], refs[-1]
    columns = blocks[0].shape[1]
    width = heads * HEAD_SIZE
    query_width = QUERY_HEADS * HEAD_SIZE
    key_width = KEY_VALUE_HEADS * HEAD_SIZE
    for r in range(nd):
        low = pl.multiple_of((index_ref[0] ^ r) * columns, HEAD_SIZE)
        whole[:, pl.ds(low, columns)] = blocks[r][...]
    for k in range(n):
        unit = (index_ref[1] ^ k) // splits
        key = unit * heads // (QUERY_HEADS // KEY_VALUE_HEADS) * HEAD_SIZE
        starts = (unit * width, query_width + key, query_width + key_width + key)
        lane = 0
        for start, size in zip(starts, (width, HEAD_SIZE, HEAD_SIZE)):
            outs[k][:, lane : lane + size] = whole[:, pl.ds(pl.multiple_of(start, HEAD_SIZE), size)]
            lane += size


def send_call(n, heads, splits, index, blocks):
    rows, columns = blocks[0].shape
    vmem = pl.BlockSpec(memory_space=pltpu.VMEM)
    wide = (heads + 2) * HEAD_SIZE
    return pl.pallas_call(
        functools.partial(send_kernel, n, heads, splits),
        out_shape=[jax.ShapeDtypeStruct((rows, wide), BF)] * n,
        in_specs=[pl.BlockSpec(memory_space=pltpu.SMEM)] + [vmem] * len(blocks),
        out_specs=[vmem] * n,
        scratch_shapes=[pltpu.VMEM((rows, columns * len(blocks)), BF)],
        compiler_params=pltpu.CompilerParams(vmem_limit_bytes=8 * 1024 * 1024),
        name="send",
    )(index, *blocks)


def lanes_kernel(splits, got_ref, out_ref):
    units, _, width = got_ref.shape
    for unit in range(0, units, splits):
        value = got_ref[unit]
        if splits > 1:
            value = value.astype(F32)
            for k in range(1, splits):
                value = value + got_ref[unit + k].astype(F32)
            value = value.astype(BF)
        low = unit // splits * width
        out_ref[:, low : low + width] = value


def lanes_call(splits, got):
    units, rows, width = got.shape
    return pl.pallas_call(
        functools.partial(lanes_kernel, splits),
        out_shape=jax.ShapeDtypeStruct((rows, units // splits * width), BF),
        compiler_params=pltpu.CompilerParams(vmem_limit_bytes=8 * 1024 * 1024),
        name="lanes",
    )(got)


def weight_kernel(places, source_ref, strips_ref, *refs):
    out_ref = refs[-1]
    started = set(range(8)) if len(refs) == len(places) + 2 else set()
    if started:
        out_ref[...] = refs[-2][...]
    for k, (block, piece) in enumerate(places):
        size = refs[k].shape[1]
        cols = slice(piece * size, (piece + 1) * size)
        term = dot(strips_ref[source_ref[block]], refs[k][...], ((0,), (0,)))
        if piece in started:
            out_ref[:, cols] += term
        else:
            out_ref[:, cols] = term
        started.add(piece)


def weight_call(places, columns, sources, strips, blocks, before):
    vmem = pl.BlockSpec(memory_space=pltpu.VMEM)
    rest = [] if before is None else [before]
    return pl.pallas_call(
        functools.partial(weight_kernel, places),
        out_shape=jax.ShapeDtypeStruct((strips.shape[2], columns), F32),
        in_specs=[pl.BlockSpec(memory_space=pltpu.SMEM)] + [vmem] * (1 + len(blocks) + len(rest)),
        out_specs=vmem,
        compiler_params=pltpu.CompilerParams(vmem_limit_bytes=24 * 1024 * 1024),
        name="weight",
    )(sources, strips, *blocks, *rest)


def project_kernel(nd, chunk, weight_ref, extra_ref, *refs):
    bases, outs, total = refs[:nd], refs[nd : 2 * nd], refs[2 * nd]
    base = bases[0].shape[0]
    extra = extra_ref.shape[0] // nd
    total[...] = jnp.zeros_like(total)

    @pl.loop(0, weight_ref.shape[0] // chunk)
    def _(step):
        part = pl.ds(pl.multiple_of(step * chunk, chunk), chunk)
        left = jnp.concatenate([ref[:, part] for ref in bases] + [extra_ref[:, part]], axis=0)
        total[...] += dot(left, weight_ref[part, :], ((1,), (0,)))

    for r in range(nd):
        low = nd * base + r * extra
        outs[r][...] = jnp.concatenate(
            [total[r * base : (r + 1) * base, :], total[low : low + extra, :]], axis=0
        ).astype(BF)


def project_call(bases, extras, weight):
    nd, (base, model), columns = len(bases), bases[0].shape, weight.shape[1]
    rows = base + extras.shape[0] // nd
    vmem = pl.BlockSpec(memory_space=pltpu.VMEM)
    return pl.pallas_call(
        functools.partial(project_kernel, nd, model // 4),
        out_shape=[jax.ShapeDtypeStruct((rows, columns), BF)] * nd,
        in_specs=[vmem] * (2 + nd),
        out_specs=[vmem] * nd,
        scratch_shapes=[pltpu.VMEM((nd * rows, columns), F32)],
        compiler_params=pltpu.CompilerParams(vmem_limit_bytes=24 * 1024 * 1024),
        name="project",
    )(weight, extras, *bases)


def rows_grad_kernel(nd, base, chunk, pieces, weight_ref, *refs):
    grad_refs, refs = refs[:pieces], refs[pieces:]
    rows, size = grad_refs[0].shape[0] // nd, grad_refs[0].shape[1]

    @pl.loop(0, weight_ref.shape[0] // chunk)
    def _(step):
        part = pl.ds(pl.multiple_of(step * chunk, chunk), chunk)
        term = None
        for k in range(pieces):
            more = dot(
                grad_refs[k][...], weight_ref[part, k * size : (k + 1) * size], ((1,), (1,))
            )
            term = more if term is None else term + more
        for r in range(nd):
            low = r * rows
            refs[r % 2][r // 2, :, part] = term[low : low + base].astype(BF)
            refs[2 + r % 2][r // 2, :, part] = term[low + base : low + rows].astype(BF)


def rows_grad_call(nd, base, extra, grads, weight):
    model, _ = weight.shape
    vmem = pl.BlockSpec(memory_space=pltpu.VMEM)
    return pl.pallas_call(
        functools.partial(rows_grad_kernel, nd, base, model // 4, len(grads)),
        out_shape=[
            jax.ShapeDtypeStruct((nd // 2, size, model), BF) for size in (base, base, extra, extra)
        ],
        in_specs=[vmem] * (1 + len(grads)),
        out_specs=[vmem] * 4,
        compiler_params=pltpu.CompilerParams(vmem_limit_bytes=24 * 1024 * 1024),
        name="rows_grad",
    )(weight, *grads)


def regroup_kernel(n, splits, width, columns, index_ref, *refs):
    outs, got_ref = refs[n:-1], refs[-1]
    units = n
    for k in range(n):
        got_ref[index_ref[1] ^ k] = refs[k][...]
    per_key = units // KEY_VALUE_HEADS
    lanes = []
    for head in range(units // splits):
        for piece in range(0, width, HEAD_SIZE):
            lanes.append((range(head * splits, (head + 1) * splits), piece))
    for offset in (width, width + HEAD_SIZE):
        for head in range(KEY_VALUE_HEADS):
            lanes.append((range(head * per_key, (head + 1) * per_key), offset))
    per_block = columns // HEAD_SIZE
    for r, out in enumerate(outs):
        for place in range(len(outs)):

            @pl.when((index_ref[0] ^ r) == place)
            def _():
                for k in range(per_block):
                    sources, lane = lanes[place * per_block + k]
                    parts = [got_ref[u, :, lane : lane + HEAD_SIZE] for u in sources]
                    value = parts[0]
                    if len(parts) > 1:
                        value = value.astype(F32)
                        for part in parts[1:]:
                            value = value + part.astype(F32)
                        value = value.astype(BF)
                    out[:, k * HEAD_SIZE : (k + 1) * HEAD_SIZE] = value


def regroup_call(splits, width, columns, nd, index, got):
    vmem = pl.BlockSpec(memory_space=pltpu.VMEM)
    n, rows, wide = len(got), *got[0].shape
    return pl.pallas_call(
        functools.partial(regroup_kernel, n, splits, width, columns),
        out_shape=[jax.ShapeDtypeStruct((rows, columns), BF)] * nd,
        in_specs=[pl.BlockSpec(memory_space=pltpu.SMEM)] + [vmem] * n,
        out_specs=[vmem] * nd,
        scratch_shapes=[pltpu.VMEM((n, rows, wide), BF)],
        compiler_params=pltpu.CompilerParams(vmem_limit_bytes=8 * 1024 * 1024),
        name="regroup",
    )(index, *got)


def body(byte_states, byte_patch, patch_owner, qkv_weight, attention_output_gradient):
    n, nd = lax.axis_size("seq"), lax.axis_size("dp")
    nx = nd // 2
    column_index = lax.axis_index("dp")
    seq_index = lax.axis_index("seq")
    ny = 1
    while 2 * (2 * ny) ** 2 <= n:
        ny *= 2
    nz = n // ny

    byte_rows = byte_states[0]
    byte_total, model = byte_rows.shape
    slot_count = byte_total // 2
    base = byte_total // 4
    owner_rows = attention_output_gradient.shape[1]
    extra = owner_rows - base
    total = patch_owner.shape[1]
    columns = qkv_weight.shape[1]

    def dp_hop(value, distance):
        return lax.ppermute(value, "dp", [(i, i ^ distance) for i in range(nd)])

    def seq_hop(value, target_of):
        return lax.ppermute(value, "seq", [(i, target_of(i)) for i in range(n)])

    def seq_swap(value):
        return lax.all_to_all(value, "seq", split_axis=0, concat_axis=0, tiled=True)

    def seq_exchange(blocks):
        if n <= 8:
            got = {k: seq_hop(blocks[k], lambda i: i ^ k) for k in range(n - 1, 0, -1)}
            return [blocks[0]] + [got[k] for k in range(1, n)]
        stacked = jnp.stack(blocks)
        order = seq_index ^ jnp.arange(n, dtype=jnp.int32)
        got = seq_swap(jnp.take(stacked, order, axis=0))
        got = jnp.take(got, order, axis=0)
        return [got[k] for k in range(n)]

    def dp_gather(value):
        blocks = [None] * nd
        blocks[0] = value
        for k in range(1, nx):
            blocks[2 * k] = dp_hop(value, 2 * k)
        for k in range(nx):
            blocks[2 * k + 1] = dp_hop(blocks[2 * k], 1)
        return blocks

    def dp_swap(blocks):
        order = sorted(range(1, nd), key=lambda r: r < 2)
        got = {r: dp_hop(blocks[r], r) for r in order}
        return [blocks[0]] + [got[r] for r in range(1, nd)]

    def dp_reduce(keep, give):
        got = dp_hop(give, 1)
        held = (keep.astype(F32) + got.astype(F32)).astype(BF)
        result = held[0].astype(F32)
        for k in range(1, nx):
            result = result + dp_hop(held[k], 2 * k).astype(F32)
        return result.astype(BF)

    patch_ids = byte_patch[0]
    first_patch = patch_ids[0]
    local_ids = patch_ids - first_patch
    slot_range = jnp.arange(slot_count, dtype=jnp.int32)
    onehot = local_ids[None, :] == slot_range[:, None]
    counts = jnp.sum(onehot.astype(F32), axis=1)
    summed = dot(onehot.astype(BF), byte_rows, ((1,), (0,)))
    pooled = (summed / jnp.maximum(counts, 1.0)[:, None]).astype(BF)
    base_rows = pooled[:base]
    spread = seq_exchange(
        [
            lax.dynamic_slice_in_dim(pooled, base + (seq_index ^ k) * extra, extra, axis=0)
            for k in range(n)
        ],
    )
    extra_rows = sum(part.astype(F32) for part in spread).astype(BF)

    base_all = dp_gather(base_rows)
    extra_all = jnp.concatenate(
        [extra_rows] + [dp_hop(extra_rows, r) for r in range(1, nd)], axis=0
    )
    if extra % 8 == 0:
        proj = project_call(base_all, extra_all, qkv_weight)
    else:
        part = dot(jnp.concatenate(base_all, axis=0), qkv_weight, ((1,), (0,))).astype(BF)
        rest = dot(extra_all, qkv_weight, ((1,), (0,))).astype(BF)
        proj = [
            jnp.concatenate(
                [part[r * base : (r + 1) * base], rest[r * extra : (r + 1) * extra]], axis=0
            )
            for r in range(nd)
        ]

    relative = dp_swap(proj)

    heads = max(1, QUERY_HEADS // n)
    splits = max(1, n // QUERY_HEADS)
    width = heads * HEAD_SIZE
    query_width = QUERY_HEADS * HEAD_SIZE

    indices = jnp.stack([column_index, seq_index]).astype(jnp.int32)
    qkvs = seq_exchange(send_call(n, heads, splits, indices, relative))

    padded = owner_rows + 1 + (-owner_rows - 1) % 16
    behind = (first_patch // base - seq_index).astype(BF)
    flags = jnp.broadcast_to(behind, (padded - owner_rows, query_width))
    cot_rows = jnp.concatenate([attention_output_gradient[0], flags], axis=0)
    cot_rows = cot_rows.reshape(padded, n // splits, width).transpose(1, 0, 2)
    cot = seq_swap(jnp.repeat(cot_rows, splits, axis=0)).reshape(n * padded, width)

    patch_range = jnp.arange(total, dtype=jnp.int32)
    group_row = patch_range // n
    target = jnp.stack(
        [
            patch_owner[0] * padded + group_row,
            patch_owner[0] * owner_rows + group_row,
        ],
        axis=1,
    )
    out_rows, *grads, spike_block = attention_call(
        n, base, extra, heads, splits, indices[1:], target, cot, qkvs
    )
    spike = spike_block[0, 0]

    out_got = seq_swap(out_rows.reshape(n, owner_rows, width))
    attn = lanes_call(splits, out_got)

    grads_got = seq_exchange(grads)
    grad_blocks = regroup_call(splits, width, columns, nd, indices, grads_got)
    swapped = dp_swap(grad_blocks)
    halves = 2 if columns % (2 * HEAD_SIZE) == 0 else 1
    size = columns // halves
    grad_cols = [
        jnp.concatenate([part[:, k * size : (k + 1) * size] for part in swapped], axis=0)
        for k in range(halves)
    ]

    if owner_rows % 8 == 0:
        base_keep, base_give, extra_keep, extra_give = rows_grad_call(
            nd, base, extra, grad_cols, qkv_weight
        )
    else:
        back = dot(jnp.concatenate(grad_cols, axis=1), qkv_weight, ((1,), (1,))).astype(BF)
        back = back.reshape(nx, 2, owner_rows, model)
        base_keep, base_give = back[:, 0, :base], back[:, 1, :base]
        extra_keep, extra_give = back[:, 0, base:], back[:, 1, base:]
    extra_grad = dp_reduce(extra_keep, extra_give)
    to_spike = (jnp.arange(n, dtype=jnp.int32) == spike)[:, None, None]
    extra_back = seq_swap(jnp.where(to_spike, extra_grad[None], jnp.zeros((), BF)))
    base_grad = dp_reduce(base_keep, base_give)
    slot_grads = jnp.concatenate([base_grad, extra_back.reshape(base, model)], axis=0)
    byte_counts = jnp.sum(jnp.where(onehot, counts[:, None], 0.0), axis=0)
    picked = dot(onehot.astype(BF), slot_grads, ((0,), (0,)))
    state_grad = (picked / jnp.maximum(byte_counts, 1.0)[:, None]).astype(BF)

    own_rows = jnp.concatenate([base_rows, extra_rows], axis=0)
    strip = model // n
    strips = seq_swap(own_rows.reshape(owner_rows, n, strip).transpose(1, 0, 2))
    all_strips = jnp.concatenate(dp_gather(strips), axis=1)
    zi, yi = seq_index // ny, seq_index % ny
    current = grad_cols
    blocks, places, sources = [], [], []
    for kz in range(nz):
        for ky in range(ny):
            for k in range(halves):
                moved = current[k]
                if ky:
                    moved = seq_hop(moved, lambda i: i // ny * ny + (i + ky) % ny)
                blocks.append(moved)
                places.append((len(sources), k))
            sources.append(((zi - kz) % nz) * ny + (yi - ky) % ny)
        if kz < nz - 1:
            current = [seq_hop(part, lambda i: (i + ny) % n) for part in current]
    sources = jnp.stack(sources).astype(jnp.int32)
    early = (len(sources) - ny) * halves
    weight_grad = weight_call(
        tuple(places[:early]), columns, sources, all_strips, blocks[:early], None
    )
    weight_grad = weight_call(
        tuple(places[early:]), columns, sources, all_strips, blocks[early:], weight_grad
    )
    return (attn[None], state_grad[None], weight_grad)


def solution(mesh):
    return jax.shard_map(
        body,
        mesh=mesh,
        in_specs=(
            P("dp", "seq", None),
            P("dp", "seq"),
            P("dp", None),
            P(None, "dp"),
            P("dp", "seq", None),
        ),
        out_specs=(P("dp", "seq", None), P("dp", "seq", None), P("seq", "dp")),
        check_vma=False,
    )
```
